32 devices in a mesh: groups: 2 (over y), seq: 16 (over z, x, core).
Axes of the slice: x: 2, y: 2, z: 4, core: 2. Of those that a mesh axis runs over, the one named last changes fastest.
Arguments:
- frames_in: bfloat16 [8192, 1024], P(('groups', 'seq')), parts along dimension 0, may hold values from -40 to 40
- rec_start: int32 [8192], P(('groups', 'seq')), parts along dimension 0, may hold values from 0 to 4095, as said below
- norm_attn: float32 [1024], replicated, may hold values from 0.1 to 1.9
- w_query: bfloat16 [1024, 1024], replicated, may hold values from -1 to 1
- w_key: bfloat16 [1024, 1024], replicated, may hold values from -1 to 1
- w_value: bfloat16 [1024, 1024], replicated, may hold values from -0.1875 to 0.1875
- w_out: bfloat16 [1024, 1024], replicated, may hold values from -0.1875 to 0.1875
- norm_conv: float32 [1024], replicated, may hold values from 0.1 to 1.9
- w_glu: bfloat16 [1024, 2048], replicated, may hold values from -0.1875 to 0.1875
- w_depth: float32 [31, 1024], replicated, may hold values from -1 to 1
- norm_depth: float32 [1024], replicated, may hold values from 0.1 to 1.9
Outputs:
- conv_out: bfloat16 [8192, 1024], P(('groups', 'seq')), parts along dimension 0
The draws below stay inside these ranges and needn't reach their ends.
There are 2 independent parts, one for each index of `groups`. The reference program is written for one: setup_inputs(seed, part) draws one part's arguments, and reference() takes and returns one part's arrays. A program takes and returns all parts, laid end to end along the dimension named above; an argument that names none is the same for every part. Nothing has to cross between parts.
Inputs may be any that keep to these rules, and one draw needn't show every extreme that they name: Recordings lie end to end from frame 0; rec_start[i] is the first frame of the recording that holds frame i. Each recording has 213 to 1280 frames, except the last, which the slab's end may cut; one of the first two has exactly 1280 frames.
All inputs are finite; a program needn't handle non-finite values.
Results may differ from the reference program's by a relative error of at most 0.0065.
Values may be sent and summed in bfloat16 or wider, within the bound.
A program may use at most 128 MiB of HBM per device.

```python
import math
import jax
import jax.numpy as jnp
from jax import lax

D = 1024
HD = 64
KW = 31
FRAMES = 256
HOPS = 5
REC_MAX = 1280
REC_MIN = 213
SLAB = 4096


LOG_TEN = 2.302585092994046


def draw_frames_in(key, part):
    key_base, key_rows, key_columns = jax.random.split(jax.random.fold_in(key, 3), 3)
    base = jax.random.truncated_normal(key_base, -4.0, 4.0, (SLAB, D), jnp.float32)
    row_scale = jnp.exp(jax.random.uniform(key_rows, (SLAB, 1), jnp.float32, 0.0, LOG_TEN))
    column_scale = jnp.exp(jax.random.uniform(key_columns, (1, D), jnp.float32, 0.0, LOG_TEN))
    return jnp.clip(base * row_scale * column_scale / 10.0, -40.0, 40.0).astype(jnp.bfloat16)


def projection_pair(key):
    key_first, key_second = jax.random.split(jax.random.fold_in(key, 101), 2)
    spread = (4.0 / D) ** 0.5
    first_matrix = jax.random.truncated_normal(key_first, -4.0, 4.0, (D, D), jnp.float32) * spread
    second_matrix = jax.random.truncated_normal(key_second, -4.0, 4.0, (D, D), jnp.float32) * spread
    return (jnp.clip(first_matrix, -1.0, 1.0), jnp.clip(second_matrix, -1.0, 1.0))


def draw_w_query(key, part):
    return projection_pair(key)[0].astype(jnp.bfloat16)


def draw_w_key(key, part):
    return projection_pair(key)[1].astype(jnp.bfloat16)


def draw_rec_start(key, part):
    record_count = SLAB // REC_MIN + 2
    key_lengths, key_longest = jax.random.split(jax.random.fold_in(key, 7))
    lengths = jax.random.randint(key_lengths, (record_count,), REC_MIN, REC_MAX + 1, jnp.int32)
    longest = jax.random.randint(key_longest, (), 0, 2, jnp.int32)
    lengths = jnp.where(jnp.arange(record_count, dtype=jnp.int32) == longest, REC_MAX, lengths)
    record_ends = jnp.cumsum(lengths)
    record_begins = record_ends - lengths
    places = jnp.arange(SLAB, dtype=jnp.int32)
    record_index = jnp.sum((record_ends[None, :] <= places[:, None]).astype(jnp.int32), axis=1)
    chosen = jnp.arange(record_count, dtype=jnp.int32)[None, :] == record_index[:, None]
    return jnp.sum(jnp.where(chosen, record_begins[None, :], 0), axis=1).astype(jnp.int32)


def bell_draw(key, extent, scale, most, kind=jnp.bfloat16):
    values = scale * jax.random.normal(key, extent, jnp.float32)
    return jnp.clip(values, min=-most, max=most).astype(kind)


def setup_inputs(seed: int = 0, part: int = 0) -> dict:
    splits = jax.random.split(jax.random.key(seed), 12)
    part_splits = jax.random.split(jax.random.fold_in(splits[11], part), 12)
    frames_in = draw_frames_in(jax.random.fold_in(jax.random.fold_in(splits[11], part), 71), part)
    rec_start = draw_rec_start(jax.random.fold_in(jax.random.fold_in(splits[11], part), 71), part)
    norm_attn = jnp.clip(1.0 + 0.18 * jax.random.normal(splits[2], (D,), jnp.float32), 0.1, 1.9)
    w_query = draw_w_query(jax.random.fold_in(splits[11], 71), part)
    w_key = draw_w_key(jax.random.fold_in(splits[11], 71), part)
    w_value = bell_draw(splits[5], (D, D), D ** -0.5, 0.1875)
    w_out = bell_draw(splits[6], (D, D), D ** -0.5, 0.1875)
    norm_conv = jnp.clip(1.0 + 0.18 * jax.random.normal(splits[7], (D,), jnp.float32), 0.1, 1.9)
    w_glu = bell_draw(splits[8], (D, 2 * D), D ** -0.5, 0.1875)
    w_depth = bell_draw(splits[9], (KW, D), KW ** -0.5, 1.0, jnp.float32)
    norm_depth = jnp.clip(1.0 + 0.18 * jax.random.normal(splits[10], (D,), jnp.float32), 0.1, 1.9)
    return {"frames_in": frames_in, "rec_start": rec_start, "norm_attn": norm_attn, "w_query": w_query, "w_key": w_key, "w_value": w_value, "w_out": w_out, "norm_conv": norm_conv, "w_glu": w_glu, "w_depth": w_depth, "norm_depth": norm_depth}


EPSILON = 1e-05
FLOOR_SCORE = -1e+30

def layer_norm(entries, scaling):
    entries = entries.astype(jnp.float32)
    center = entries - lax.optimization_barrier(jnp.mean(entries, axis=-1, keepdims=True))
    spread = lax.optimization_barrier(jnp.mean(center * center, axis=-1, keepdims=True))
    return center * lax.rsqrt(spread + EPSILON) * scaling.astype(jnp.float32)

def gated_units(features, norm_conv, w_glu):
    normed_conv = layer_norm(features, norm_conv).astype(jnp.bfloat16)
    mixed = jnp.dot(normed_conv, w_glu, preferred_element_type=jnp.float32)
    feature_width = features.shape[1]
    return (mixed[:, :feature_width] * jax.nn.sigmoid(mixed[:, feature_width:])).astype(jnp.bfloat16)

def reference(frames_in, rec_start, norm_attn, w_query, w_key, w_value, w_out, norm_conv, w_glu, w_depth, norm_depth):
    head_count = D // HD
    normed_in = layer_norm(frames_in, norm_attn).astype(jnp.bfloat16)
    query = jnp.dot(normed_in, w_query, preferred_element_type=jnp.float32).astype(jnp.bfloat16)
    key_rows = jnp.dot(normed_in, w_key, preferred_element_type=jnp.float32).astype(jnp.bfloat16)
    value_rows = jnp.dot(normed_in, w_value, preferred_element_type=jnp.float32).astype(jnp.bfloat16)
    reach = HOPS * FRAMES
    window = reach + FRAMES
    front_zeros = jnp.zeros((reach, D), jnp.bfloat16)
    keys_long = jnp.concatenate([front_zeros, key_rows], axis=0)
    values_long = jnp.concatenate([front_zeros, value_rows], axis=0)
    score_scale = 1.0 / math.sqrt(HD)

    def attend_block(block_index):
        begin = block_index * FRAMES
        query_heads = lax.dynamic_slice_in_dim(query, begin, FRAMES, 0).astype(jnp.float32).reshape(FRAMES, head_count, HD)
        key_heads = lax.dynamic_slice_in_dim(keys_long, begin, window, 0).astype(jnp.float32).reshape(window, head_count, HD)
        value_heads = lax.dynamic_slice_in_dim(values_long, begin, window, 0).astype(jnp.float32).reshape(window, head_count, HD)
        starts = lax.dynamic_slice_in_dim(rec_start, begin, FRAMES, 0)
        query_places = begin + jnp.arange(FRAMES, dtype=jnp.int32)
        key_places = begin - reach + jnp.arange(window, dtype=jnp.int32)
        visible = (key_places[None, :] >= starts[:, None]) & (key_places[None, :] <= query_places[:, None])
        scores = jnp.einsum('qhd,khd->hqk', query_heads, key_heads) * score_scale
        highest = lax.optimization_barrier(jnp.max(jnp.where(visible[None], scores, FLOOR_SCORE), axis=-1, keepdims=True))
        weights = jnp.where(visible[None], jnp.exp(scores - highest), 0.0).astype(jnp.bfloat16)
        weight_sum = lax.optimization_barrier(jnp.sum(weights.astype(jnp.float32), axis=-1))
        summed = jnp.einsum('hqk,khd->qhd', weights.astype(jnp.float32), value_heads)
        return (summed / weight_sum.T[:, :, None]).reshape(FRAMES, D).astype(jnp.bfloat16)
    heads_out = lax.map(attend_block, jnp.arange(SLAB // FRAMES, dtype=jnp.int32)).reshape(SLAB, D)
    attn_res = (frames_in.astype(jnp.float32) + jnp.dot(heads_out, w_out, preferred_element_type=jnp.float32)).astype(jnp.bfloat16)
    gated = gated_units(attn_res, norm_conv, w_glu)
    padded = jnp.concatenate([jnp.zeros((KW - 1, D), jnp.bfloat16), gated], axis=0)
    places = jnp.arange(SLAB, dtype=jnp.int32)
    depth = jnp.zeros((SLAB, D), jnp.float32)
    for tap_index in range(KW):
        source = places - (KW - 1) + tap_index
        keep = (source >= rec_start)[:, None]
        depth = depth + jnp.where(keep, padded[tap_index:tap_index + SLAB].astype(jnp.float32), 0.0) * w_depth[tap_index].astype(jnp.float32)
    normed_depth = layer_norm(depth, norm_depth)
    return (attn_res.astype(jnp.float32) + normed_depth * jax.nn.sigmoid(normed_depth)).astype(jnp.bfloat16)
```

```python
import jax
import jax.numpy as jnp
from jax import lax
from jax.experimental import pallas as pl
from jax.experimental.pallas import tpu as pltpu
from jax.sharding import PartitionSpec as P

HD = 64
KW = 31
EPSILON = 1e-05
FLOOR_SCORE = -1e30
F32 = jnp.float32
BF16 = jnp.bfloat16
MESH = pl.DeviceIdType.MESH
PIECES = 4
UNROLL = 8
TILE = 512
GROUPS = ((0, 1), (1, 1), (2, 2), (4, 1))
PLACE = {4: 0, 2: 1, 1: 2, 3: 3, 5: 4}
DISTANCE = (4, 2, 1, 3, 5)
A, B, C, D, E, F, G, H, I = range(9)


def layer_norm(entries, scaling):
    center = entries - jnp.mean(entries, axis=-1, keepdims=True)
    spread = jnp.mean(center * center, axis=-1, keepdims=True)
    return center * lax.rsqrt(spread + EPSILON) * scaling


def kernel(
    x_hbm, start_hbm, na_hbm, nc_hbm, nd_hbm, wd_hbm,
    wq_hbm, wk_hbm, wv_hbm, wo_hbm, wg_hbm,
    out_ref,
    xb, own, qx, kx, wq, wk, wv, wo, wg, xn, q2, kb, vb, bias_own, startb, mx, acc, heads,
    res, gb, halo, planes, depth, taps,
    x_ref, start_ref, na_ref, nc_ref, nd_ref, wd_ref, kinds,
    w_sem, in_sem, send_sem, recv_sem, halo_sem,
):
    n = lax.axis_size("seq")
    me = lax.axis_index("seq")
    p = me % 4
    rows, width = x_ref.shape
    piece = rows // PIECES
    pairs = width // 128
    span = rows + 32

    frames = [
        pltpu.make_async_copy(
            x_hbm.at[pl.ds(part * piece, piece)], x_ref.at[pl.ds(part * piece, piece)],
            in_sem.at[part],
        )
        for part in range(PIECES)
    ]
    small = [
        pltpu.make_async_copy(src, dst, in_sem.at[PIECES + index])
        for index, (src, dst) in enumerate((
            (na_hbm, na_ref), (start_hbm, start_ref), (nc_hbm, nc_ref), (nd_hbm, nd_ref),
            (wd_hbm, wd_ref),
        ))
    ]
    small[0].start()
    for copy in frames:
        copy.start()
    for copy in small[1:]:
        copy.start()

    barrier = pltpu.get_barrier_semaphore()
    peers = jnp.int32(0)
    for delta in (-4, -3, -2, -1, 1, 2, 3, 4):
        inside = (me + delta >= 0) & (me + delta < n)
        peers = peers + jnp.where(inside, 1, 0)

        @pl.when(inside)
        def _():
            pl.semaphore_signal(
                barrier, inc=1, device_id={"seq": me + delta}, device_id_type=MESH
            )

    weights = [
        pltpu.make_async_copy(src, dst, w_sem.at[index])
        for index, (src, dst) in enumerate(
            ((wq_hbm, wq), (wk_hbm, wk), (wv_hbm, wv), (wo_hbm, wo), (wg_hbm, wg))
        )
    ]
    for copy in weights:
        copy.start()

    def move(event, part, source, target, distance):
        part_rows = pl.ds(part * piece, piece)
        src = own.at[part_rows] if source is None else xb.at[PLACE[source], part_rows]
        return pltpu.make_async_remote_copy(
            src_ref=src,
            dst_ref=xb.at[PLACE[distance], part_rows],
            send_sem=send_sem.at[event, part],
            recv_sem=recv_sem.at[event, part],
            device_id={"seq": target},
            device_id_type=MESH,
        )

    even = p % 2 == 0
    sends = {
        A: [(me + 4 < n, None, me + 4, 4)],
        B: [(p < 2, None, me + 2, 2)],
        C: [(even, None, me + 1, 1)],
        D: [(p == 2, 2, me + 1, 3), (p == 3, 2, me - 1, 1)],
        E: [((me >= 4) & even, 4, me + 1, 5), ((me >= 4) & (p % 2 == 1), 4, me - 1, 3)],
        F: [((me >= 4) & (p >= 2), 4, me - 2, 2)],
        G: [((me >= 4) & (p == 0), 2, me + 1, 3), ((me >= 4) & (p == 1), 2, me - 1, 1)],
        H: [((p == 3) & (me + 3 < n), 2, me + 3, 5)],
        I: [((me >= 4) & (p == 1) & (me + 3 < n), 2, me + 3, 5)],
    }
    receipts = {
        A: [(me >= 4, 4)],
        B: [(p >= 2, 2)],
        C: [(p % 2 == 1, 1)],
        D: [(p == 3, 3), (p == 2, 1)],
        E: [((me >= 4) & (p % 2 == 1), 5), ((me >= 4) & even, 3)],
        F: [((me >= 4) & (p < 2), 2)],
        G: [((me >= 4) & (p == 1), 3), ((me >= 4) & (p == 0), 1)],
        H: [((me >= 4) & (p == 2), 5)],
        I: [((me >= 8) & (p == 0), 5)],
    }

    def start(event, part):
        for condition, source, target, distance in sends[event]:
            @pl.when(condition)
            def _():
                move(event, part, source, target, distance).start()

    def wait_sent(event, part):
        for condition, source, target, distance in sends[event]:
            @pl.when(condition)
            def _():
                move(event, part, source, target, distance).wait_send()

    def wait_here(event, part):
        for condition, distance in receipts[event]:
            @pl.when(condition)
            def _():
                move(event, part, None, me, distance).wait_recv()

    small[0].wait()
    gain = na_ref[...]
    for part in range(PIECES):
        frames[part].wait()
        own[part * piece:(part + 1) * piece, :] = layer_norm(
            x_ref[part * piece:(part + 1) * piece, :].astype(F32), gain
        ).astype(BF16)
        if part == 0:
            pl.semaphore_wait(barrier, peers)
        start(A, part)
        start(B, part)
    for part in range(PIECES):
        start(C, part)

    for distance in DISTANCE:
        @pl.when(me < distance)
        def _():
            xb[PLACE[distance]] = jnp.zeros((rows, width), BF16)

    for copy in small[1:]:
        copy.wait()
    for tile in range(pairs):
        taps[pl.ds(tile, KW, stride=8), :] = wd_ref[:, tile * 128:(tile + 1) * 128]

    column = jnp.broadcast_to(start_ref[...].astype(F32), (rows, rows)).T
    startb[...] = column[:, :128] - (me * rows).astype(F32)
    first = startb[...]
    middle = first == jnp.broadcast_to(startb[128:129, :], (rows, 128))
    for tile in range(8):
        kinds[pl.ds(tile, rows, stride=8), :] = jnp.where(middle, 1.0, 0.0)
    lane = lax.broadcasted_iota(jnp.int32, (rows, 128), 1).astype(F32)
    row_index = lax.broadcasted_iota(jnp.int32, (rows, 128), 0).astype(F32)
    for tile in range(rows // 128):
        place = lane + float(tile * 128)
        seen = (place >= first) & (place <= row_index)
        bias_own[:, tile * 128:(tile + 1) * 128] = jnp.where(seen, 0.0, FLOOR_SCORE)

    head = jnp.broadcast_to(startb[0:1, :], (rows, 128))
    flags = jnp.where(
        lane == 0.0, jnp.where(first == head, 0.0, FLOOR_SCORE), jnp.where(lane == 1.0, 1.0, 0.0)
    ).astype(BF16)
    qx[0:rows, :] = flags
    qx[rows:2 * rows, :] = flags
    for slot, distance in enumerate(DISTANCE):
        hidden = jnp.where(row_index - float(distance * rows) >= head, 0.0, FLOOR_SCORE)
        kx[slot * rows:(slot + 1) * rows, :] = jnp.where(
            lane == 0.0, 1.0, jnp.where(lane == 1.0, hidden, 0.0)
        ).astype(BF16)

    def key_values(source, count):
        def column_tile(index, carry):
            cols = pl.ds(pl.multiple_of(index * TILE, TILE), TILE)
            normed = source()
            kb[0:count * rows, cols] = jnp.dot(
                normed, wk[:, cols], preferred_element_type=F32
            ).astype(BF16)
            vb[0:count * rows, cols] = jnp.dot(
                normed, wv[:, cols], preferred_element_type=F32
            ).astype(BF16)
            return carry

        lax.fori_loop(0, width // TILE, column_tile, 0)

    def attend(slot, count):
        keys = count * rows
        opening = slot is None

        def pair_step(pair, carry):
            cols = pl.ds(pl.multiple_of(pair * 128, 128), 128)
            query, key = q2[:, cols], kb[0:keys, cols]
            if not opening:
                query = jnp.concatenate([query, qx[...]], axis=1)
                key = jnp.concatenate([key, kx[slot * rows:slot * rows + keys, :]], axis=1)
            scores = lax.dot_general(
                query, key, (((1,), (1,)), ((), ())), preferred_element_type=F32
            )
            if opening:
                shade = bias_own[...]
                scores = scores + jnp.concatenate([shade, shade], axis=0)
            top = jnp.broadcast_to(
                jnp.max(scores, axis=-1, keepdims=True), (2 * rows, 128)
            )
            if not opening:
                before = mx[pair]
                top = jnp.maximum(top, before)
            weights16 = jnp.exp(scores - jnp.tile(top, (1, keys // 128))).astype(BF16)
            values = jnp.concatenate(
                [vb[0:keys, cols], jnp.ones((keys, 128), BF16)], axis=1
            )
            summed = jnp.dot(weights16, values, preferred_element_type=F32)
            if not opening:
                summed = summed + acc[pair] * jnp.tile(jnp.exp(before - top), (1, 2))
            acc[pair] = summed
            mx[pair] = top
            return carry

        lax.fori_loop(0, pairs, pair_step, 0, unroll=UNROLL)

    weights[0].wait()

    def query_tile(index, carry):
        cols = pl.ds(pl.multiple_of(index * 256, 256), 256)
        query = jnp.dot(own[...], wq[:, cols], preferred_element_type=F32)
        query = query.astype(BF16).astype(F32) * (HD ** -0.5)
        low = lax.broadcasted_iota(jnp.int32, (rows, 256), 1) % 128 < HD
        q2[0:rows, cols] = jnp.where(low, query, 0.0).astype(BF16)
        q2[rows:2 * rows, cols] = jnp.where(low, 0.0, query).astype(BF16)
        return carry

    lax.fori_loop(0, width // 256, query_tile, 0)
    weights[1].wait()
    weights[2].wait()
    key_values(lambda: own[...], 1)

    def relay_first(part):
        wait_here(B, part)
        start(D, part)
        start(H, part)
        wait_here(A, part)
        start(F, part)
        start(E, part)

    def relay_second(part):
        wait_here(F, part)
        start(I, part)
        start(G, part)

    relay_first(0)
    attend(None, 1)
    for part in range(1, PIECES):
        relay_first(part)

    def remote(slot, count):
        key_values(
            lambda: xb[slot:slot + count].reshape(count * rows, width), count
        )
        attend(slot, count)

    for turn, (slot, count) in enumerate(GROUPS):
        if turn == 1:
            for part in range(PIECES):
                relay_second(part)
        arrivals = {2: (C, D, E, G), 3: (H, I)} if len(GROUPS) == 4 else {2: (C, D, E, G, H, I)}
        if turn in arrivals:
            for event in arrivals[turn]:
                for part in range(PIECES):
                    wait_here(event, part)
        remote(slot, count)

    low = lax.broadcasted_iota(jnp.int32, (rows, 128), 1) < HD

    def close_pair(pair, carry):
        cols = pl.ds(pl.multiple_of(pair * 128, 128), 128)
        state = acc[pair]
        total = jnp.where(low, state[0:rows, 0:128], state[rows:2 * rows, 0:128])
        weight_sum = jnp.where(low, state[0:rows, 128:256], state[rows:2 * rows, 128:256])
        heads[:, cols] = (total / weight_sum).astype(BF16)
        return carry

    lax.fori_loop(0, pairs, close_pair, 0)
    weights[3].wait()

    def output_tile(index, carry):
        cols = pl.ds(pl.multiple_of(index * 256, 256), 256)
        res[:, cols] = (
            x_ref[:, cols].astype(F32)
            + jnp.dot(heads[...], wo[:, cols], preferred_element_type=F32)
        ).astype(BF16)
        return carry

    lax.fori_loop(0, width // 256, output_tile, 0)
    xn[0:rows, :] = layer_norm(res[...].astype(F32), nc_ref[...]).astype(BF16)
    weights[4].wait()

    def unit_tile(index, carry):
        cols = pl.ds(pl.multiple_of(index * 256, 256), 256)
        gate_cols = pl.ds(pl.multiple_of(width + index * 256, 256), 256)
        normed = xn[0:rows, :]
        value = jnp.dot(normed, wg[:, cols], preferred_element_type=F32)
        gate = jnp.dot(normed, wg[:, gate_cols], preferred_element_type=F32)
        gated = (value * jax.nn.sigmoid(gate)).astype(BF16)
        gb[:, cols] = gated
        middle = startb[...] == jnp.broadcast_to(startb[128:129, :], (rows, 128))
        for half in range(2):
            units = gated[:, half * 128:(half + 1) * 128].astype(F32)
            place = 32 * 8 + index * 2 + half
            planes[pl.ds(place, rows, stride=8), :] = jnp.where(middle, 0.0, units)
            planes[pl.ds(span * 8 + place, rows, stride=8), :] = jnp.where(middle, units, 0.0)
        return carry

    lax.fori_loop(0, width // 256, unit_tile, 0)

    rim = pltpu.make_async_remote_copy(
        src_ref=gb.at[pl.ds(rows - 32, 32)],
        dst_ref=halo,
        send_sem=halo_sem.at[0],
        recv_sem=halo_sem.at[1],
        device_id={"seq": me + 1},
        device_id_type=MESH,
    )

    @pl.when(me + 1 < n)
    def _():
        rim.start()

    block = 16

    def conv_block(index, carry):
        base = index * block

        def row(ref, place):
            return ref[pl.ds(pl.multiple_of(place * 8, 8), 8), :]

        inside = [row(kinds, base + r) > 0.5 for r in range(block)]
        total = [None] * block
        for j in range(KW - 1):
            place = base + 2 + j
            entry = jnp.where(inside[0], row(planes, span + place), row(planes, place))
            for r in range(min(j + 1, block)):
                term = entry * tap_rows[j - r]
                total[r] = term if total[r] is None else total[r] + term
        for r in range(1, block):
            total[r] = jnp.where(inside[r] == inside[0], total[r], 0.0)
        for j in range(block):
            place = base + 32 + j
            other, middle = row(planes, place), row(planes, span + place)
            for r in range(j, block):
                entry = jnp.where(inside[r], middle, other)
                total[r] = total[r] + entry * tap_rows[KW - 1 - r + j]
        for r in range(block):
            depth[pl.ds(pl.multiple_of((base + r) * 8, 8), 8), :] = total[r]
        return carry

    tap_rows = [taps[tap * 8:(tap + 1) * 8, :] for tap in range(KW)]
    lax.fori_loop(2, rows // block, conv_block, 0)

    def finish(low_row, count):
        columns = [
            depth[pl.ds(low_row * 8 + tile, count, stride=8), :] for tile in range(pairs)
        ]
        normed_depth = layer_norm(jnp.concatenate(columns, axis=1), nd_ref[...])
        out_ref[low_row:low_row + count, :] = (
            res[low_row:low_row + count, :].astype(F32)
            + normed_depth * jax.nn.sigmoid(normed_depth)
        ).astype(BF16)

    finish(32, rows - 32)

    @pl.when(me == 0)
    def _():
        halo[...] = jnp.zeros_like(halo)

    @pl.when(me > 0)
    def _():
        rim.wait_recv()

    back = lax.broadcasted_iota(jnp.int32, (32, 128), 0).astype(F32) - 32.0
    middle = back >= jnp.broadcast_to(startb[128:129, :], (32, 128))
    for tile in range(pairs):
        units = halo[:, tile * 128:(tile + 1) * 128].astype(F32)
        planes[pl.ds(tile, 32, stride=8), :] = jnp.where(middle, 0.0, units)
        planes[pl.ds(span * 8 + tile, 32, stride=8), :] = jnp.where(middle, units, 0.0)
    lax.fori_loop(0, 2, conv_block, 0)
    finish(0, 32)

    for event in range(9):
        for part in range(PIECES):
            wait_sent(event, part)

    @pl.when(me + 1 < n)
    def _():
        rim.wait_send()


def body(
    frames_in, rec_start, norm_attn, w_query, w_key, w_value, w_out, norm_conv, w_glu, w_depth,
    norm_depth,
):
    rows, width = frames_in.shape
    pairs = width // 128
    vmem = pl.BlockSpec(memory_space=pltpu.VMEM)
    hbm = pl.BlockSpec(memory_space=pl.ANY)
    square = pltpu.VMEM((width, width), BF16)
    return pl.pallas_call(
        kernel,
        out_shape=pltpu.VMEM((rows, width), BF16),
        in_specs=[hbm] * 11,
        out_specs=vmem,
        scratch_shapes=[
            pltpu.VMEM((5, rows, width), BF16),
            pltpu.VMEM((rows, width), BF16),
            pltpu.VMEM((2 * rows, 128), BF16),
            pltpu.VMEM((5 * rows, 128), BF16),
            square, square, square, square,
            pltpu.VMEM((width, 2 * width), BF16),
            pltpu.VMEM((rows, width), BF16),
            pltpu.VMEM((2 * rows, width), BF16),
            pltpu.VMEM((3 * rows, width), BF16),
            pltpu.VMEM((3 * rows, width), BF16),
            pltpu.VMEM((rows, rows), F32),
            pltpu.VMEM((rows, 128), F32),
            pltpu.VMEM((pairs, 2 * rows, 128), F32),
            pltpu.VMEM((pairs, 2 * rows, 256), F32),
            pltpu.VMEM((rows, width), BF16),
            pltpu.VMEM((rows, width), BF16),
            pltpu.VMEM((rows, width), BF16),
            pltpu.VMEM((32, width), BF16),
            pltpu.VMEM((2 * (rows + 32) * 8, 128), F32),
            pltpu.VMEM((rows * 8, 128), F32),
            pltpu.VMEM((KW * 8, 128), F32),
            pltpu.VMEM((rows, width), BF16),
            pltpu.VMEM((1, rows), jnp.int32),
            pltpu.VMEM((1, width), F32),
            pltpu.VMEM((1, width), F32),
            pltpu.VMEM((1, width), F32),
            pltpu.VMEM((KW, width), F32),
            pltpu.VMEM((rows * 8, 128), F32),
            pltpu.SemaphoreType.DMA((5,)),
            pltpu.SemaphoreType.DMA((PIECES + 5,)),
            pltpu.SemaphoreType.DMA((9, PIECES)),
            pltpu.SemaphoreType.DMA((9, PIECES)),
            pltpu.SemaphoreType.DMA((2,)),
        ],
        compiler_params=pltpu.CompilerParams(
            collective_id=0, has_side_effects=True, vmem_limit_bytes=60 * 1024 * 1024
        ),
    )(
        frames_in, rec_start.reshape(1, rows), norm_attn.reshape(1, width),
        norm_conv.reshape(1, width), norm_depth.reshape(1, width), w_depth,
        w_query, w_key, w_value, w_out, w_glu,
    )


def solution(mesh):
    return jax.shard_map(
        body,
        mesh=mesh,
        in_specs=(P(("groups", "seq"), None), P(("groups", "seq"))) + (P(),) * 9,
        out_specs=P(("groups", "seq"), None),
        check_vma=False,
    )
```

```python
import jax
import jax.numpy as jnp
from jax import lax
from jax.experimental import pallas as pl
from jax.experimental.pallas import tpu as pltpu
from jax.sharding import PartitionSpec as P

HD = 64
KW = 31
EPSILON = 1e-05
FLOOR_SCORE = -1e30
F32 = jnp.float32
BF16 = jnp.bfloat16
MESH = pl.DeviceIdType.MESH
PIECES = 4
A, B, D, E, F, H, I, S = range(8)
OWN, FAR, NEAR, LAST = range(4)


def layer_norm(entries, scaling):
    center = entries - jnp.mean(entries, axis=-1, keepdims=True)
    spread = jnp.mean(center * center, axis=-1, keepdims=True)
    return center * lax.rsqrt(spread + EPSILON) * scaling


def kernel(
    x_hbm, start_hbm, na_hbm, nc_hbm, nd_hbm, wd_hbm,
    wq_hbm, wk_hbm, wv_hbm, wo_hbm, wg_hbm,
    out_ref,
    xb, qx, kx, wq, wk, wv, wo, wg, xn, q2, kb, vb, triangle, startb, startc, mx, acc,
    heads, heads_in, partial, res, gb, halo, planes, depth, taps,
    x_ref, start_ref, na_ref, nc_ref, nd_ref, wd_ref, kinds,
    w_sem, in_sem, send_sem, recv_sem, halo_sem, start_sem, heads_send, heads_recv,
):
    n = lax.axis_size("seq")
    me = lax.axis_index("seq")
    p = me % 4
    k = me % 2
    sibling = me + 1 - 2 * k
    upper = me >= 4
    right = p >= 2
    rows, width = x_ref.shape
    piece = rows // PIECES
    pairs = width // 128
    half = width // 2
    own_pairs = half // 128
    span = rows + 32

    frames = [
        pltpu.make_async_copy(
            x_hbm.at[pl.ds(part * piece, piece)], x_ref.at[pl.ds(part * piece, piece)],
            in_sem.at[part],
        )
        for part in range(PIECES)
    ]
    small = [
        pltpu.make_async_copy(src, dst, in_sem.at[PIECES + index])
        for index, (src, dst) in enumerate((
            (na_hbm, na_ref), (start_hbm, start_ref.at[k]), (nc_hbm, nc_ref), (nd_hbm, nd_ref),
            (wd_hbm, wd_ref),
        ))
    ]
    small[0].start()
    for copy in frames:
        copy.start()
    small[1].start()

    barrier = pltpu.get_barrier_semaphore()
    peers = jnp.int32(0)
    for delta in (-4, -2, -1, 1, 2, 4):
        inside = (me + delta >= 0) & (me + delta < n)
        peers = peers + jnp.where(inside, 1, 0)

        @pl.when(inside)
        def _():
            pl.semaphore_signal(
                barrier, inc=1, device_id={"seq": me + delta}, device_id_type=MESH
            )

    mine = pl.ds(pl.multiple_of(k * half, 128), half)
    weights = [
        pltpu.make_async_copy(src, dst, w_sem.at[index])
        for index, (src, dst) in enumerate((
            (wq_hbm.at[:, mine], wq), (wk_hbm.at[:, mine], wk), (wv_hbm.at[:, mine], wv),
            (wo_hbm, wo), (wg_hbm, wg),
        ))
    ]
    for copy in weights[:3]:
        copy.start()
    for copy in small[2:]:
        copy.start()
    for copy in weights[3:]:
        copy.start()

    def place_of(section, core, part):
        if section == OWN:
            return core * rows + part * piece
        if section == LAST:
            return 6 * rows + part * piece
        return (section * 2 + part // 2) * rows + core * 2 * piece + part % 2 * piece

    def move(event, part, source, target, section, core):
        def block(where):
            low_row = place_of(where, core, part)
            return xb.at[pl.ds(pl.multiple_of(low_row, 16), piece)]

        return pltpu.make_async_remote_copy(
            src_ref=block(source),
            dst_ref=block(section),
            send_sem=send_sem.at[event, part],
            recv_sem=recv_sem.at[event, part],
            device_id={"seq": target},
            device_id_type=MESH,
        )

    sends = {
        S: (me >= 0, OWN, sibling, OWN),
        A: (me + 4 < n, OWN, me + 4, FAR),
        B: (p < 2, OWN, me + 2, NEAR),
        D: (me >= 2, NEAR, sibling, NEAR),
        E: (upper, FAR, sibling, FAR),
        F: (upper & right, FAR, me - 2, NEAR),
        H: ((k == 1) & (me >= 2) & (me + 4 < n), NEAR, me + 4, LAST),
        I: ((k == 1) & (me >= 6), LAST, sibling, LAST),
    }
    receipts = {
        S: (me >= 0, OWN),
        A: (upper, FAR),
        B: (right, NEAR),
        D: (me >= 2, NEAR),
        E: (upper, FAR),
        F: (upper & (p < 2), NEAR),
        H: ((k == 1) & (me >= 6), LAST),
        I: ((k == 0) & (me >= 6), LAST),
    }

    def start(event, part):
        condition, source, target, section = sends[event]

        @pl.when(condition)
        def _():
            move(event, part, source, target, section, k).start()

    def wait_sent(event, part):
        condition, source, target, section = sends[event]

        @pl.when(condition)
        def _():
            move(event, part, source, target, section, k).wait_send()

    def wait_here(event, part):
        condition, section = receipts[event]
        core = 1 - k if event in (S, D, E, I) else k

        @pl.when(condition)
        def _():
            move(event, part, section, sibling, section, core).wait_recv()

    starts = pltpu.make_async_remote_copy(
        src_ref=start_ref.at[k],
        dst_ref=start_ref.at[k],
        send_sem=start_sem.at[0],
        recv_sem=start_sem.at[1],
        device_id={"seq": sibling},
        device_id_type=MESH,
    )

    small[0].wait()
    gain = na_ref[...]
    for part in range(PIECES):
        frames[part].wait()
        low_row = pl.multiple_of(place_of(OWN, k, part), 16)
        xb[pl.ds(low_row, piece), :] = layer_norm(
            x_ref[part * piece:(part + 1) * piece, :].astype(F32), gain
        ).astype(BF16)
        if part == 0:
            pl.semaphore_wait(barrier, peers)
        start(A, part)
        start(B, part)
        start(S, part)
        if part == 0:
            small[1].wait()
            starts.start()

    @pl.when(me < 2)
    def _():
        xb[4 * rows:6 * rows, :] = jnp.zeros((2 * rows, width), BF16)

    @pl.when(me < 4)
    def _():
        xb[2 * rows:4 * rows, :] = jnp.zeros((2 * rows, width), BF16)

    @pl.when(me < 6)
    def _():
        xb[6 * rows:7 * rows, :] = jnp.zeros((rows, width), BF16)

    lane = lax.broadcasted_iota(jnp.int32, (rows, 128), 1).astype(F32)
    row_index = lax.broadcasted_iota(jnp.int32, (rows, 128), 0).astype(F32)
    low = lax.broadcasted_iota(jnp.int32, (rows, 128), 1) < HD
    for tile in range(rows // 128):
        seen = lane + float(tile * 128) <= row_index
        triangle[:, tile * 128:(tile + 1) * 128] = jnp.where(seen, 0.0, FLOOR_SCORE)

    def project(core):
        span_rows = pl.ds(pl.multiple_of(core * rows, 256), rows)
        normed = xb[span_rows, :]
        query = jnp.dot(normed, wq[...], preferred_element_type=F32)
        query = query.astype(BF16).astype(F32) * (HD ** -0.5)
        wide = lax.broadcasted_iota(jnp.int32, (rows, half), 1) % 128 < HD
        place = pl.multiple_of(core * 2 * rows, 256)
        q2[pl.ds(place, rows), :] = jnp.where(wide, query, 0.0).astype(BF16)
        q2[pl.ds(place + rows, rows), :] = jnp.where(wide, 0.0, query).astype(BF16)
        kb[span_rows, :] = jnp.dot(normed, wk[...], preferred_element_type=F32).astype(BF16)
        vb[span_rows, :] = jnp.dot(normed, wv[...], preferred_element_type=F32).astype(BF16)

    for copy in weights[:3]:
        copy.wait()
    project(k)

    starts.wait_recv()
    for core in range(2):
        column = jnp.broadcast_to(start_ref[core].astype(F32), (rows, rows)).T
        startb[core * rows:(core + 1) * rows, :] = (
            column[:, :128] - ((me - k) * rows).astype(F32)
        )
    startc[...] = startb[pl.ds(pl.multiple_of(k * rows, 256), rows), :] - (k * rows).astype(F32)
    for core in range(2):
        first = startb[core * rows:(core + 1) * rows, :]
        bucket = jnp.where(first < 0.0, 4.0, jnp.floor(first * (1.0 / 128.0)))
        flags = jnp.where(lane == bucket, 1.0, 0.0).astype(BF16)
        qx[core * 2 * rows:(core * 2 + 1) * rows, :] = flags
        qx[(core * 2 + 1) * rows:(core * 2 + 2) * rows, :] = flags
        kx[core * rows:(core + 1) * rows, :] = jnp.where(
            (lane == bucket) | (lane > 4.0), 0.0, FLOOR_SCORE
        ).astype(BF16)
    head = jnp.broadcast_to(startb[0:1, :], (rows, 128))

    def remote_flags(back):
        return jnp.where(
            lane < 4.0, FLOOR_SCORE,
            jnp.where((lane == 4.0) & (back < head), FLOOR_SCORE, 0.0),
        ).astype(BF16)

    for section, distance in ((FAR, 4), (NEAR, 2)):
        for part in range(2):
            back = row_index + float(part * 2 * piece - distance * rows)
            back = jnp.where(row_index >= float(2 * piece), back + float(2 * piece), back)
            place = (section * 2 + part) * rows
            kx[place:place + rows, :] = remote_flags(back)
    kx[6 * rows:7 * rows, :] = remote_flags(row_index - float(5 * rows))

    middle = startc[...] == jnp.broadcast_to(startc[128:129, :], (rows, 128))
    for tile in range(8):
        kinds[pl.ds(tile, rows, stride=8), :] = jnp.where(middle, 1.0, 0.0)

    for part in range(PIECES):
        wait_here(S, part)
    project(1 - k)

    def attend(low_query, queries, low_key, keys, opening):
        for pair in range(own_pairs):
            cols = slice(pair * 128, (pair + 1) * 128)
            held = slice(low_query, low_query + queries)
            spot = slice(low_key, low_key + keys)
            query = jnp.concatenate([q2[held, cols], qx[held, :]], axis=1)
            key = jnp.concatenate([kb[spot, cols], kx[spot, :]], axis=1)
            scores = lax.dot_general(
                query, key, (((1,), (1,)), ((), ())), preferred_element_type=F32
            )
            if opening:
                shade = triangle[...]
                if keys > rows:
                    shade = jnp.concatenate([jnp.zeros((rows, keys - rows), F32), shade], axis=1)
                scores = scores + jnp.concatenate([shade, shade], axis=0)
            top = jnp.broadcast_to(jnp.max(scores, axis=-1, keepdims=True), (queries, 128))
            if not opening:
                before = mx[pair, held]
                top = jnp.maximum(top, before)
            weights16 = jnp.exp(scores - jnp.tile(top, (1, keys // 128))).astype(BF16)
            values = jnp.concatenate([vb[spot, cols], jnp.ones((keys, 128), BF16)], axis=1)
            summed = jnp.dot(weights16, values, preferred_element_type=F32)
            if not opening:
                summed = summed + acc[pair, held] * jnp.tile(jnp.exp(before - top), (1, 2))
            acc[pair, held] = summed
            mx[pair, held] = top

    def relay_first(part):
        wait_here(A, part)
        start(F, part)
        start(E, part)
        wait_here(B, part)

        @pl.when(right)
        def _():
            move(D, part, NEAR, sibling, NEAR, k).start()
        condition, source, target, section = sends[H]

        @pl.when(right & condition)
        def _():
            move(H, part, source, target, section, k).start()

    def relay_second(part):
        wait_here(F, part)

        @pl.when(upper & (p < 2))
        def _():
            move(D, part, NEAR, sibling, NEAR, k).start()
        condition, source, target, section = sends[H]

        @pl.when(upper & (p < 2) & condition)
        def _():
            move(H, part, source, target, section, k).start()

    def relay_third(part):
        wait_here(H, part)
        start(I, part)

    def keys_of(group):
        spot = slice(group * rows, (group + 1) * rows)
        normed = xb[spot, :]
        kb[spot, :] = jnp.dot(normed, wk[...], preferred_element_type=F32).astype(BF16)
        vb[spot, :] = jnp.dot(normed, wv[...], preferred_element_type=F32).astype(BF16)

    def arrived(event, parts):
        for part in parts:
            wait_here(event, part)

    attend(0, 2 * rows, 0, rows, True)
    relay_first(0)
    attend(2 * rows, 2 * rows, 0, 2 * rows, True)
    relay_first(1)
    relay_second(0)
    arrived(E, (0, 1))
    keys_of(2)
    relay_first(2)
    relay_second(1)
    attend(0, 4 * rows, 2 * rows, rows, False)
    arrived(D, (0, 1))
    keys_of(4)
    relay_first(3)
    relay_second(2)
    attend(0, 4 * rows, 4 * rows, rows, False)
    arrived(E, (2, 3))
    keys_of(3)
    relay_second(3)
    relay_third(0)
    attend(0, 4 * rows, 3 * rows, rows, False)
    arrived(D, (2, 3))
    keys_of(5)
    relay_third(1)
    attend(0, 4 * rows, 5 * rows, rows, False)

    def heads_copy(core, pair):
        cols = pl.ds(pair * 128, 128)
        return pltpu.make_async_remote_copy(
            src_ref=heads.at[core, :, cols],
            dst_ref=heads_in.at[:, cols],
            send_sem=heads_send.at[pair],
            recv_sem=heads_recv.at[pair],
            device_id={"seq": sibling},
            device_id_type=MESH,
        )

    def close(core):
        for pair in range(own_pairs):
            cols = slice(pair * 128, (pair + 1) * 128)
            state = acc[pair, core * 2 * rows:(core + 1) * 2 * rows]
            total = jnp.where(low, state[0:rows, 0:128], state[rows:2 * rows, 0:128])
            weight_sum = jnp.where(low, state[0:rows, 128:256], state[rows:2 * rows, 128:256])
            heads[core, :, cols] = (total / weight_sum).astype(BF16)

            @pl.when(k != core)
            def _():
                heads_copy(core, pair).start()

    relay_third(2)
    close(1)
    relay_third(3)
    arrived(I, range(PIECES))
    keys_of(6)
    attend(0, 2 * rows, 6 * rows, rows, False)
    close(0)
    weights[3].wait()
    for copy in small[2:]:
        copy.wait()
    for tile in range(pairs):
        taps[pl.ds(tile, KW, stride=8), :] = wd_ref[:, tile * 128:(tile + 1) * 128]

    def output_near(index, carry):
        cols = pl.ds(pl.multiple_of(index * half, half), half)
        here = pl.ds(pl.multiple_of(k * half, half), half)
        partial[:, cols] = x_ref[:, cols].astype(F32) + jnp.dot(
            heads[k], wo[here, cols], preferred_element_type=F32
        )
        return carry

    lax.fori_loop(0, 2, output_near, 0, unroll=True)
    for pair in range(own_pairs):
        heads_copy(1 - k, pair).wait_recv()

    def output_far(index, carry):
        cols = pl.ds(pl.multiple_of(index * half, half), half)
        there = pl.ds(pl.multiple_of((1 - k) * half, half), half)
        res[:, cols] = (
            partial[:, cols]
            + jnp.dot(heads_in[...], wo[there, cols], preferred_element_type=F32)
        ).astype(BF16)
        return carry

    lax.fori_loop(0, 2, output_far, 0, unroll=True)
    xn[...] = layer_norm(res[...].astype(F32), nc_ref[...]).astype(BF16)
    weights[4].wait()

    def unit_tile(index, carry):
        cols = pl.ds(pl.multiple_of(index * 256, 256), 256)
        gate_cols = pl.ds(pl.multiple_of(width + index * 256, 256), 256)
        normed = xn[...]
        value = jnp.dot(normed, wg[:, cols], preferred_element_type=F32)
        gate = jnp.dot(normed, wg[:, gate_cols], preferred_element_type=F32)
        gated = (value * jax.nn.sigmoid(gate)).astype(BF16)
        gb[:, cols] = gated
        middle = startc[...] == jnp.broadcast_to(startc[128:129, :], (rows, 128))
        for side in range(2):
            units = gated[:, side * 128:(side + 1) * 128].astype(F32)
            place = 32 * 8 + index * 2 + side
            planes[pl.ds(place, rows, stride=8), :] = jnp.where(middle, 0.0, units)
            planes[pl.ds(span * 8 + place, rows, stride=8), :] = jnp.where(middle, units, 0.0)
        return carry

    lax.fori_loop(0, width // 256, unit_tile, 0)

    rim = pltpu.make_async_remote_copy(
        src_ref=gb.at[pl.ds(rows - 32, 32)],
        dst_ref=halo,
        send_sem=halo_sem.at[0],
        recv_sem=halo_sem.at[1],
        device_id={"seq": me + 1},
        device_id_type=MESH,
    )

    @pl.when(me + 1 < n)
    def _():
        rim.start()

    block = 16

    def conv_block(index, carry):
        base = index * block

        def row(ref, place):
            return ref[pl.ds(pl.multiple_of(place * 8, 8), 8), :]

        inside = [row(kinds, base + r) > 0.5 for r in range(block)]
        total = [None] * block
        for j in range(KW - 1):
            place = base + 2 + j
            entry = jnp.where(inside[0], row(planes, span + place), row(planes, place))
            for r in range(min(j + 1, block)):
                term = entry * tap_rows[j - r]
                total[r] = term if total[r] is None else total[r] + term
        for r in range(1, block):
            total[r] = jnp.where(inside[r] == inside[0], total[r], 0.0)
        for j in range(block):
            place = base + 32 + j
            other, middle = row(planes, place), row(planes, span + place)
            for r in range(j, block):
                entry = jnp.where(inside[r], middle, other)
                total[r] = total[r] + entry * tap_rows[KW - 1 - r + j]
        for r in range(block):
            depth[pl.ds(pl.multiple_of((base + r) * 8, 8), 8), :] = total[r]
        return carry

    tap_rows = [taps[tap * 8:(tap + 1) * 8, :] for tap in range(KW)]
    lax.fori_loop(2, rows // block, conv_block, 0)

    def finish(low_row, count):
        columns = [
            depth[pl.ds(low_row * 8 + tile, count, stride=8), :] for tile in range(pairs)
        ]
        normed_depth = layer_norm(jnp.concatenate(columns, axis=1), nd_ref[...])
        out_ref[low_row:low_row + count, :] = (
            res[low_row:low_row + count, :].astype(F32)
            + normed_depth * jax.nn.sigmoid(normed_depth)
        ).astype(BF16)

    finish(32, rows - 32)

    @pl.when(me == 0)
    def _():
        halo[...] = jnp.zeros_like(halo)

    @pl.when(me > 0)
    def _():
        rim.wait_recv()

    back = lax.broadcasted_iota(jnp.int32, (32, 128), 0).astype(F32) - 32.0
    middle = back >= jnp.broadcast_to(startc[128:129, :], (32, 128))
    for tile in range(pairs):
        units = halo[:, tile * 128:(tile + 1) * 128].astype(F32)
        planes[pl.ds(tile, 32, stride=8), :] = jnp.where(middle, 0.0, units)
        planes[pl.ds(span * 8 + tile, 32, stride=8), :] = jnp.where(middle, units, 0.0)
    lax.fori_loop(0, 2, conv_block, 0)
    finish(0, 32)

    for event in range(8):
        for part in range(PIECES):
            wait_sent(event, part)
    starts.wait_send()
    for pair in range(own_pairs):
        heads_copy(1 - k, pair).wait_send()

    @pl.when(me + 1 < n)
    def _():
        rim.wait_send()


def body(
    frames_in, rec_start, norm_attn, w_query, w_key, w_value, w_out, norm_conv, w_glu, w_depth,
    norm_depth,
):
    rows, width = frames_in.shape
    half = width // 2
    own_pairs = half // 128
    hbm = pl.BlockSpec(memory_space=pl.ANY)
    tall = pltpu.VMEM((width, half), BF16)
    return pl.pallas_call(
        kernel,
        out_shape=pltpu.VMEM((rows, width), BF16),
        in_specs=[hbm] * 11,
        out_specs=pl.BlockSpec(memory_space=pltpu.VMEM),
        scratch_shapes=[
            pltpu.VMEM((7 * rows, width), BF16),
            pltpu.VMEM((4 * rows, 128), BF16),
            pltpu.VMEM((7 * rows, 128), BF16),
            tall, tall, tall,
            pltpu.VMEM((width, width), BF16),
            pltpu.VMEM((width, 2 * width), BF16),
            pltpu.VMEM((rows, width), BF16),
            pltpu.VMEM((4 * rows, half), BF16),
            pltpu.VMEM((7 * rows, half), BF16),
            pltpu.VMEM((7 * rows, half), BF16),
            pltpu.VMEM((rows, rows), F32),
            pltpu.VMEM((2 * rows, 128), F32),
            pltpu.VMEM((rows, 128), F32),
            pltpu.VMEM((own_pairs, 4 * rows, 128), F32),
            pltpu.VMEM((own_pairs, 4 * rows, 256), F32),
            pltpu.VMEM((2, rows, half), BF16),
            pltpu.VMEM((rows, half), BF16),
            pltpu.VMEM((rows, width), F32),
            pltpu.VMEM((rows, width), BF16),
            pltpu.VMEM((rows, width), BF16),
            pltpu.VMEM((32, width), BF16),
            pltpu.VMEM((2 * (rows + 32) * 8, 128), F32),
            pltpu.VMEM((rows * 8, 128), F32),
            pltpu.VMEM((KW * 8, 128), F32),
            pltpu.VMEM((rows, width), BF16),
            pltpu.VMEM((2, 1, rows), jnp.int32),
            pltpu.VMEM((1, width), F32),
            pltpu.VMEM((1, width), F32),
            pltpu.VMEM((1, width), F32),
            pltpu.VMEM((KW, width), F32),
            pltpu.VMEM((rows * 8, 128), F32),
            pltpu.SemaphoreType.DMA((5,)),
            pltpu.SemaphoreType.DMA((PIECES + 5,)),
            pltpu.SemaphoreType.DMA((8, PIECES)),
            pltpu.SemaphoreType.DMA((8, PIECES)),
            pltpu.SemaphoreType.DMA((2,)),
            pltpu.SemaphoreType.DMA((2,)),
            pltpu.SemaphoreType.DMA((own_pairs,)),
            pltpu.SemaphoreType.DMA((own_pairs,)),
        ],
        compiler_params=pltpu.CompilerParams(
            collective_id=0, has_side_effects=True, vmem_limit_bytes=60 * 1024 * 1024
        ),
    )(
        frames_in, rec_start.reshape(1, rows), norm_attn.reshape(1, width),
        norm_conv.reshape(1, width), norm_depth.reshape(1, width), w_depth,
        w_query, w_key, w_value, w_out, w_glu,
    )


def solution(mesh):
    return jax.shard_map(
        body,
        mesh=mesh,
        in_specs=(P(("groups", "seq"), None), P(("groups", "seq"))) + (P(),) * 9,
        out_specs=P(("groups", "seq"), None),
        check_vma=False,
    )
```

```python
import jax
import jax.numpy as jnp
from jax import lax
from jax.experimental import pallas as pl
from jax.experimental.pallas import tpu as pltpu
from jax.sharding import PartitionSpec as P

HD = 64
KW = 31
EPSILON = 1e-05
FLOOR_SCORE = -1e30
F32 = jnp.float32
BF16 = jnp.bfloat16
MESH = pl.DeviceIdType.MESH
PIECES = 4
A, B, D, E, F, H, I, S = range(8)
OWN, FAR, NEAR, LAST = range(4)


def layer_norm(entries, scaling):
    center = entries - jnp.mean(entries, axis=-1, keepdims=True)
    spread = jnp.mean(center * center, axis=-1, keepdims=True)
    return center * lax.rsqrt(spread + EPSILON) * scaling


def kernel(
    x_hbm, start_hbm, na_hbm, nc_hbm, nd_hbm, wd_hbm,
    wq_hbm, wk_hbm, wv_hbm, wo_hbm, wg_hbm,
    out_ref,
    xb, qx, kx, wq, wk, wv, wo, wg, xn, q2, kb, vb, triangle, startb, startc, mx, acc,
    heads, heads_in, partial, res, gb, halo, planes, depth, taps,
    x_ref, start_ref, na_ref, nc_ref, nd_ref, wd_ref, kinds,
    w_sem, in_sem, send_sem, recv_sem, halo_sem, start_sem, heads_send, heads_recv,
):
    n = lax.axis_size("seq")
    me = lax.axis_index("seq")
    p = me % 4
    k = me % 2
    sibling = me + 1 - 2 * k
    upper = me >= 4
    right = p >= 2
    rows, width = x_ref.shape
    piece = rows // PIECES
    pairs = width // 128
    half = width // 2
    own_pairs = half // 128
    span = rows + 32

    frames = [
        pltpu.make_async_copy(
            x_hbm.at[pl.ds(part * piece, piece)], x_ref.at[pl.ds(part * piece, piece)],
            in_sem.at[part],
        )
        for part in range(PIECES)
    ]
    small = [
        pltpu.make_async_copy(src, dst, in_sem.at[PIECES + index])
        for index, (src, dst) in enumerate((
            (na_hbm, na_ref), (start_hbm, start_ref.at[k]), (nc_hbm, nc_ref), (nd_hbm, nd_ref),
            (wd_hbm, wd_ref),
        ))
    ]
    small[0].start()
    for copy in frames:
        copy.start()
    small[1].start()

    barrier = pltpu.get_barrier_semaphore()
    peers = jnp.int32(0)
    for delta in (-4, -2, -1, 1, 2, 4):
        inside = (me + delta >= 0) & (me + delta < n)
        peers = peers + jnp.where(inside, 1, 0)

        @pl.when(inside)
        def _():
            pl.semaphore_signal(
                barrier, inc=1, device_id={"seq": me + delta}, device_id_type=MESH
            )

    mine = pl.ds(pl.multiple_of(k * half, 128), half)
    weights = [
        pltpu.make_async_copy(src, dst, w_sem.at[index])
        for index, (src, dst) in enumerate((
            (wq_hbm.at[:, mine], wq), (wk_hbm.at[:, mine], wk), (wv_hbm.at[:, mine], wv),
            (wo_hbm, wo), (wg_hbm, wg),
        ))
    ]
    for copy in weights[:3]:
        copy.start()
    for copy in small[2:]:
        copy.start()
    for copy in weights[3:]:
        copy.start()

    def place_of(section, core, part):
        if section == OWN:
            return core * rows + part * piece
        if section == LAST:
            return 6 * rows + part * piece
        return (section * 2 + part // 2) * rows + core * 2 * piece + part % 2 * piece

    def move(event, part, source, target, section, core):
        def block(where):
            low_row = place_of(where, core, part)
            return xb.at[pl.ds(pl.multiple_of(low_row, 16), piece)]

        return pltpu.make_async_remote_copy(
            src_ref=block(source),
            dst_ref=block(section),
            send_sem=send_sem.at[event, part],
            recv_sem=recv_sem.at[event, part],
            device_id={"seq": target},
            device_id_type=MESH,
        )

    sends = {
        S: (me >= 0, OWN, sibling, OWN),
        A: (me + 4 < n, OWN, me + 4, FAR),
        B: (p < 2, OWN, me + 2, NEAR),
        D: (me >= 2, NEAR, sibling, NEAR),
        E: (upper, FAR, sibling, FAR),
        F: (upper & right, FAR, me - 2, NEAR),
        H: ((k == 1) & (me >= 2) & (me + 4 < n), NEAR, me + 4, LAST),
        I: ((k == 1) & (me >= 6), LAST, sibling, LAST),
    }
    receipts = {
        S: (me >= 0, OWN),
        A: (upper, FAR),
        B: (right, NEAR),
        D: (me >= 2, NEAR),
        E: (upper, FAR),
        F: (upper & (p < 2), NEAR),
        H: ((k == 1) & (me >= 6), LAST),
        I: ((k == 0) & (me >= 6), LAST),
    }

    def start(event, part):
        condition, source, target, section = sends[event]

        @pl.when(condition)
        def _():
            move(event, part, source, target, section, k).start()

    def wait_sent(event, part):
        condition, source, target, section = sends[event]

        @pl.when(condition)
        def _():
            move(event, part, source, target, section, k).wait_send()

    def wait_here(event, part):
        condition, section = receipts[event]
        core = 1 - k if event in (S, D, E, I) else k

        @pl.when(condition)
        def _():
            move(event, part, section, sibling, section, core).wait_recv()

    starts = pltpu.make_async_remote_copy(
        src_ref=start_ref.at[k],
        dst_ref=start_ref.at[k],
        send_sem=start_sem.at[0],
        recv_sem=start_sem.at[1],
        device_id={"seq": sibling},
        device_id_type=MESH,
    )

    small[0].wait()
    gain = na_ref[...]
    for part in range(PIECES):
        frames[part].wait()
        low_row = pl.multiple_of(place_of(OWN, k, part), 16)
        xb[pl.ds(low_row, piece), :] = layer_norm(
            x_ref[part * piece:(part + 1) * piece, :].astype(F32), gain
        ).astype(BF16)
        if part == 0:
            pl.semaphore_wait(barrier, peers)
        start(A, part)
        start(B, part)
        start(S, part)
        if part == 0:
            small[1].wait()
            starts.start()

    @pl.when(me < 2)
    def _():
        xb[4 * rows:6 * rows, :] = jnp.zeros((2 * rows, width), BF16)

    @pl.when(me < 4)
    def _():
        xb[2 * rows:4 * rows, :] = jnp.zeros((2 * rows, width), BF16)

    @pl.when(me < 6)
    def _():
        xb[6 * rows:7 * rows, :] = jnp.zeros((rows, width), BF16)

    lane = lax.broadcasted_iota(jnp.int32, (rows, 128), 1).astype(F32)
    row_index = lax.broadcasted_iota(jnp.int32, (rows, 128), 0).astype(F32)
    low = lax.broadcasted_iota(jnp.int32, (rows, 128), 1) < HD
    for tile in range(rows // 128):
        seen = lane + float(tile * 128) <= row_index
        triangle[:, tile * 128:(tile + 1) * 128] = jnp.where(seen, 0.0, FLOOR_SCORE)

    def project(core):
        span_rows = pl.ds(pl.multiple_of(core * rows, 256), rows)
        normed = xb[span_rows, :]
        query = jnp.dot(normed, wq[...], preferred_element_type=F32)
        query = query.astype(BF16).astype(F32) * (HD ** -0.5)
        wide = lax.broadcasted_iota(jnp.int32, (rows, half), 1) % 128 < HD
        place = pl.multiple_of(core * 2 * rows, 256)
        q2[pl.ds(place, rows), :] = jnp.where(wide, query, 0.0).astype(BF16)
        q2[pl.ds(place + rows, rows), :] = jnp.where(wide, 0.0, query).astype(BF16)
        kb[span_rows, :] = jnp.dot(normed, wk[...], preferred_element_type=F32).astype(BF16)
        vb[span_rows, :] = jnp.dot(normed, wv[...], preferred_element_type=F32).astype(BF16)

    for copy in weights[:3]:
        copy.wait()
    project(k)

    starts.wait_recv()
    for core in range(2):
        column = jnp.broadcast_to(start_ref[core].astype(F32), (rows, rows)).T
        startb[core * rows:(core + 1) * rows, :] = (
            column[:, :128] - ((me - k) * rows).astype(F32)
        )
    startc[...] = startb[pl.ds(pl.multiple_of(k * rows, 256), rows), :] - (k * rows).astype(F32)
    for core in range(2):
        first = startb[core * rows:(core + 1) * rows, :]
        bucket = jnp.where(first < 0.0, 4.0, jnp.floor(first * (1.0 / 128.0)))
        flags = jnp.where(lane == bucket, 1.0, 0.0).astype(BF16)
        qx[core * 2 * rows:(core * 2 + 1) * rows, :] = flags
        qx[(core * 2 + 1) * rows:(core * 2 + 2) * rows, :] = flags
        kx[core * rows:(core + 1) * rows, :] = jnp.where(
            (lane == bucket) | (lane > 4.0), 0.0, FLOOR_SCORE
        ).astype(BF16)
    head = jnp.broadcast_to(startb[0:1, :], (rows, 128))

    def remote_flags(back):
        return jnp.where(
            lane < 4.0, FLOOR_SCORE,
            jnp.where((lane == 4.0) & (back < head), FLOOR_SCORE, 0.0),
        ).astype(BF16)

    for section, distance in ((FAR, 4), (NEAR, 2)):
        for part in range(2):
            back = row_index + float(part * 2 * piece - distance * rows)
            back = jnp.where(row_index >= float(2 * piece), back + float(2 * piece), back)
            place = (section * 2 + part) * rows
            kx[place:place + rows, :] = remote_flags(back)
    kx[6 * rows:7 * rows, :] = remote_flags(row_index - float(5 * rows))

    middle = startc[...] == jnp.broadcast_to(startc[128:129, :], (rows, 128))
    for tile in range(8):
        kinds[pl.ds(tile, rows, stride=8), :] = jnp.where(middle, 1.0, 0.0)

    for part in range(PIECES):
        wait_here(S, part)
    project(1 - k)

    def attend(low_query, queries, low_key, keys, opening):
        for pair in range(own_pairs):
            cols = slice(pair * 128, (pair + 1) * 128)
            held = slice(low_query, low_query + queries)
            spot = slice(low_key, low_key + keys)
            query = jnp.concatenate([q2[held, cols], qx[held, :]], axis=1)
            key = jnp.concatenate([kb[spot, cols], kx[spot, :]], axis=1)
            scores = lax.dot_general(
                query, key, (((1,), (1,)), ((), ())), preferred_element_type=F32
            )
            if opening:
                shade = triangle[...]
                if keys > rows:
                    shade = jnp.concatenate([jnp.zeros((rows, keys - rows), F32), shade], axis=1)
                scores = scores + jnp.concatenate([shade, shade], axis=0)
            top = jnp.broadcast_to(jnp.max(scores, axis=-1, keepdims=True), (queries, 128))
            if not opening:
                before = mx[pair, held]
                top = jnp.maximum(top, before)
            weights16 = jnp.exp(scores - jnp.tile(top, (1, keys // 128))).astype(BF16)
            values = jnp.concatenate([vb[spot, cols], jnp.ones((keys, 128), BF16)], axis=1)
            summed = jnp.dot(weights16, values, preferred_element_type=F32)
            if not opening:
                summed = summed + acc[pair, held] * jnp.tile(jnp.exp(before - top), (1, 2))
            acc[pair, held] = summed
            mx[pair, held] = top

    def relay_first(part):
        wait_here(A, part)
        start(F, part)
        start(E, part)
        wait_here(B, part)

        @pl.when(right)
        def _():
            move(D, part, NEAR, sibling, NEAR, k).start()
        condition, source, target, section = sends[H]

        @pl.when(right & condition)
        def _():
            move(H, part, source, target, section, k).start()

    def relay_second(part):
        wait_here(F, part)

        @pl.when(upper & (p < 2))
        def _():
            move(D, part, NEAR, sibling, NEAR, k).start()
        condition, source, target, section = sends[H]

        @pl.when(upper & (p < 2) & condition)
        def _():
            move(H, part, source, target, section, k).start()

    def relay_third(part):
        wait_here(H, part)
        start(I, part)

    def keys_of(group):
        spot = slice(group * rows, (group + 1) * rows)
        normed = xb[spot, :]
        kb[spot, :] = jnp.dot(normed, wk[...], preferred_element_type=F32).astype(BF16)
        vb[spot, :] = jnp.dot(normed, wv[...], preferred_element_type=F32).astype(BF16)

    def arrived(event, parts):
        for part in parts:
            wait_here(event, part)

    attend(0, 2 * rows, 0, rows, True)
    relay_first(0)
    attend(2 * rows, 2 * rows, 0, 2 * rows, True)
    relay_first(1)
    relay_second(0)
    arrived(E, (0, 1))
    keys_of(2)
    relay_first(2)
    relay_second(1)
    attend(0, 4 * rows, 2 * rows, rows, False)
    arrived(D, (0, 1))
    keys_of(4)
    relay_first(3)
    relay_second(2)
    attend(0, 4 * rows, 4 * rows, rows, False)
    arrived(E, (2, 3))
    keys_of(3)
    relay_second(3)
    relay_third(0)
    attend(0, 4 * rows, 3 * rows, rows, False)
    arrived(D, (2, 3))
    keys_of(5)
    relay_third(1)
    attend(0, 4 * rows, 5 * rows, rows, False)

    def heads_copy(core, pair):
        cols = pl.ds(pair * 128, 128)
        return pltpu.make_async_remote_copy(
            src_ref=heads.at[core, :, cols],
            dst_ref=heads_in.at[:, cols],
            send_sem=heads_send.at[pair],
            recv_sem=heads_recv.at[pair],
            device_id={"seq": sibling},
            device_id_type=MESH,
        )

    def close(core):
        for pair in range(own_pairs):
            cols = slice(pair * 128, (pair + 1) * 128)
            state = acc[pair, core * 2 * rows:(core + 1) * 2 * rows]
            total = jnp.where(low, state[0:rows, 0:128], state[rows:2 * rows, 0:128])
            weight_sum = jnp.where(low, state[0:rows, 128:256], state[rows:2 * rows, 128:256])
            heads[core, :, cols] = (total / weight_sum).astype(BF16)

            @pl.when(k != core)
            def _():
                heads_copy(core, pair).start()

    relay_third(2)
    close(1)
    relay_third(3)
    arrived(I, range(PIECES))
    keys_of(6)
    attend(0, 2 * rows, 6 * rows, rows, False)
    close(0)
    weights[3].wait()
    for copy in small[2:]:
        copy.wait()
    for tile in range(pairs):
        taps[pl.ds(tile, KW, stride=8), :] = wd_ref[:, tile * 128:(tile + 1) * 128]

    def output_near(index, carry):
        cols = pl.ds(pl.multiple_of(index * half, half), half)
        here = pl.ds(pl.multiple_of(k * half, half), half)
        partial[:, cols] = x_ref[:, cols].astype(F32) + jnp.dot(
            heads[k], wo[here, cols], preferred_element_type=F32
        )
        return carry

    lax.fori_loop(0, 2, output_near, 0, unroll=True)
    for pair in range(own_pairs):
        heads_copy(1 - k, pair).wait_recv()

    def output_far(index, carry):
        cols = pl.ds(pl.multiple_of(index * half, half), half)
        there = pl.ds(pl.multiple_of((1 - k) * half, half), half)
        res[:, cols] = (
            partial[:, cols]
            + jnp.dot(heads_in[...], wo[there, cols], preferred_element_type=F32)
        ).astype(BF16)
        return carry

    lax.fori_loop(0, 2, output_far, 0, unroll=True)
    xn[...] = layer_norm(res[...].astype(F32), nc_ref[...]).astype(BF16)
    weights[4].wait()

    def unit_tile(index, carry):
        cols = pl.ds(pl.multiple_of(index * 256, 256), 256)
        gate_cols = pl.ds(pl.multiple_of(width + index * 256, 256), 256)
        normed = xn[...]
        value = jnp.dot(normed, wg[:, cols], preferred_element_type=F32)
        gate = jnp.dot(normed, wg[:, gate_cols], preferred_element_type=F32)
        gated = (value * jax.nn.sigmoid(gate)).astype(BF16)
        gb[:, cols] = gated
        middle = startc[...] == jnp.broadcast_to(startc[128:129, :], (rows, 128))
        for side in range(2):
            units = gated[:, side * 128:(side + 1) * 128].astype(F32)
            place = 32 * 8 + index * 2 + side
            planes[pl.ds(place, rows, stride=8), :] = jnp.where(middle, 0.0, units)
            planes[pl.ds(span * 8 + place, rows, stride=8), :] = jnp.where(middle, units, 0.0)
        return carry

    lax.fori_loop(0, width // 256, unit_tile, 0, unroll=True)

    rim = pltpu.make_async_remote_copy(
        src_ref=gb.at[pl.ds(rows - 32, 32)],
        dst_ref=halo,
        send_sem=halo_sem.at[0],
        recv_sem=halo_sem.at[1],
        device_id={"seq": me + 1},
        device_id_type=MESH,
    )

    @pl.when(me + 1 < n)
    def _():
        rim.start()

    block = 16

    def conv_block(index, carry):
        base = index * block

        def row(ref, place):
            return ref[pl.ds(pl.multiple_of(place * 8, 8), 8), :]

        inside = [row(kinds, base + r) > 0.5 for r in range(block)]
        total = [None] * block
        for j in range(KW - 1):
            place = base + 2 + j
            entry = jnp.where(inside[0], row(planes, span + place), row(planes, place))
            for r in range(min(j + 1, block)):
                term = entry * tap_rows[j - r]
                total[r] = term if total[r] is None else total[r] + term
        for r in range(1, block):
            total[r] = jnp.where(inside[r] == inside[0], total[r], 0.0)
        for j in range(block):
            place = base + 32 + j
            other, middle = row(planes, place), row(planes, span + place)
            for r in range(j, block):
                entry = jnp.where(inside[r], middle, other)
                total[r] = total[r] + entry * tap_rows[KW - 1 - r + j]
        for r in range(block):
            depth[pl.ds(pl.multiple_of((base + r) * 8, 8), 8), :] = total[r]
        return carry

    tap_rows = [taps[tap * 8:(tap + 1) * 8, :] for tap in range(KW)]
    lax.fori_loop(2, rows // block, conv_block, 0)

    def finish(low_row, count):
        columns = [
            depth[pl.ds(low_row * 8 + tile, count, stride=8), :] for tile in range(pairs)
        ]
        normed_depth = layer_norm(jnp.concatenate(columns, axis=1), nd_ref[...])
        out_ref[low_row:low_row + count, :] = (
            res[low_row:low_row + count, :].astype(F32)
            + normed_depth * jax.nn.sigmoid(normed_depth)
        ).astype(BF16)

    finish(32, rows - 32)

    @pl.when(me == 0)
    def _():
        halo[...] = jnp.zeros_like(halo)

    @pl.when(me > 0)
    def _():
        rim.wait_recv()

    back = lax.broadcasted_iota(jnp.int32, (32, 128), 0).astype(F32) - 32.0
    middle = back >= jnp.broadcast_to(startc[128:129, :], (32, 128))
    for tile in range(pairs):
        units = halo[:, tile * 128:(tile + 1) * 128].astype(F32)
        planes[pl.ds(tile, 32, stride=8), :] = jnp.where(middle, 0.0, units)
        planes[pl.ds(span * 8 + tile, 32, stride=8), :] = jnp.where(middle, units, 0.0)
    lax.fori_loop(0, 2, conv_block, 0)
    finish(0, 32)

    for event in range(8):
        for part in range(PIECES):
            wait_sent(event, part)
    starts.wait_send()
    for pair in range(own_pairs):
        heads_copy(1 - k, pair).wait_send()

    @pl.when(me + 1 < n)
    def _():
        rim.wait_send()


def body(
    frames_in, rec_start, norm_attn, w_query, w_key, w_value, w_out, norm_conv, w_glu, w_depth,
    norm_depth,
):
    rows, width = frames_in.shape
    half = width // 2
    own_pairs = half // 128
    hbm = pl.BlockSpec(memory_space=pl.ANY)
    tall = pltpu.VMEM((width, half), BF16)
    return pl.pallas_call(
        kernel,
        out_shape=pltpu.VMEM((rows, width), BF16),
        in_specs=[hbm] * 11,
        out_specs=pl.BlockSpec(memory_space=pltpu.VMEM),
        scratch_shapes=[
            pltpu.VMEM((7 * rows, width), BF16),
            pltpu.VMEM((4 * rows, 128), BF16),
            pltpu.VMEM((7 * rows, 128), BF16),
            tall, tall, tall,
            pltpu.VMEM((width, width), BF16),
            pltpu.VMEM((width, 2 * width), BF16),
            pltpu.VMEM((rows, width), BF16),
            pltpu.VMEM((4 * rows, half), BF16),
            pltpu.VMEM((7 * rows, half), BF16),
            pltpu.VMEM((7 * rows, half), BF16),
            pltpu.VMEM((rows, rows), F32),
            pltpu.VMEM((2 * rows, 128), F32),
            pltpu.VMEM((rows, 128), F32),
            pltpu.VMEM((own_pairs, 4 * rows, 128), F32),
            pltpu.VMEM((own_pairs, 4 * rows, 256), F32),
            pltpu.VMEM((2, rows, half), BF16),
            pltpu.VMEM((rows, half), BF16),
            pltpu.VMEM((rows, width), F32),
            pltpu.VMEM((rows, width), BF16),
            pltpu.VMEM((rows, width), BF16),
            pltpu.VMEM((32, width), BF16),
            pltpu.VMEM((2 * (rows + 32) * 8, 128), F32),
            pltpu.VMEM((rows * 8, 128), F32),
            pltpu.VMEM((KW * 8, 128), F32),
            pltpu.VMEM((rows, width), BF16),
            pltpu.VMEM((2, 1, rows), jnp.int32),
            pltpu.VMEM((1, width), F32),
            pltpu.VMEM((1, width), F32),
            pltpu.VMEM((1, width), F32),
            pltpu.VMEM((KW, width), F32),
            pltpu.VMEM((rows * 8, 128), F32),
            pltpu.SemaphoreType.DMA((5,)),
            pltpu.SemaphoreType.DMA((PIECES + 5,)),
            pltpu.SemaphoreType.DMA((8, PIECES)),
            pltpu.SemaphoreType.DMA((8, PIECES)),
            pltpu.SemaphoreType.DMA((2,)),
            pltpu.SemaphoreType.DMA((2,)),
            pltpu.SemaphoreType.DMA((own_pairs,)),
            pltpu.SemaphoreType.DMA((own_pairs,)),
        ],
        compiler_params=pltpu.CompilerParams(
            collective_id=0, has_side_effects=True, vmem_limit_bytes=60 * 1024 * 1024
        ),
    )(
        frames_in, rec_start.reshape(1, rows), norm_attn.reshape(1, width),
        norm_conv.reshape(1, width), norm_depth.reshape(1, width), w_depth,
        w_query, w_key, w_value, w_out, w_glu,
    )


def solution(mesh):
    return jax.shard_map(
        body,
        mesh=mesh,
        in_specs=(P(("groups", "seq"), None), P(("groups", "seq"))) + (P(),) * 9,
        out_specs=P(("groups", "seq"), None),
        check_vma=False,
    )
```

```python
import jax
import jax.numpy as jnp
from jax import lax
from jax.experimental import pallas as pl
from jax.experimental.pallas import tpu as pltpu
from jax.sharding import PartitionSpec as P

HD = 64
KW = 31
EPSILON = 1e-05
FLOOR_SCORE = -1e30
F32 = jnp.float32
BF16 = jnp.bfloat16
MESH = pl.DeviceIdType.MESH
PIECES = 4
A, B, D, E, F, H, I, S = range(8)
OWN, FAR, NEAR, LAST = range(4)


def layer_norm(entries, scaling):
    center = entries - jnp.mean(entries, axis=-1, keepdims=True)
    spread = jnp.mean(center * center, axis=-1, keepdims=True)
    return center * lax.rsqrt(spread + EPSILON) * scaling


def kernel(
    x_hbm, start_hbm, na_hbm, nc_hbm, nd_hbm, wd_hbm,
    wq_hbm, wk_hbm, wv_hbm, wo_hbm, wg_hbm,
    out_ref,
    xb, qx, kx, wq, wk, wv, wo, wg, xn, q2, kb, vb, triangle, startb, startc, mx, acc,
    heads, heads_in, partial, res, gb, halo, planes, depth, taps,
    x_ref, start_ref, na_ref, nc_ref, nd_ref, wd_ref, kinds,
    w_sem, in_sem, send_sem, recv_sem, halo_sem, start_sem, heads_send, heads_recv,
):
    n = lax.axis_size("seq")
    me = lax.axis_index("seq")
    p = me % 4
    k = me % 2
    sibling = me + 1 - 2 * k
    upper = me >= 4
    right = p >= 2
    rows, width = x_ref.shape
    piece = rows // PIECES
    pairs = width // 128
    half = width // 2
    own_pairs = half // 128
    span = rows + 32

    frames = [
        pltpu.make_async_copy(
            x_hbm.at[pl.ds(part * piece, piece)], x_ref.at[pl.ds(part * piece, piece)],
            in_sem.at[part],
        )
        for part in range(PIECES)
    ]
    small = [
        pltpu.make_async_copy(src, dst, in_sem.at[PIECES + index])
        for index, (src, dst) in enumerate((
            (na_hbm, na_ref), (start_hbm, start_ref.at[k]), (nc_hbm, nc_ref), (nd_hbm, nd_ref),
            (wd_hbm, wd_ref),
        ))
    ]
    small[0].start()
    for copy in frames:
        copy.start()
    small[1].start()

    barrier = pltpu.get_barrier_semaphore()
    peers = jnp.int32(0)
    for delta in (-4, -2, -1, 1, 2, 4):
        inside = (me + delta >= 0) & (me + delta < n)
        peers = peers + jnp.where(inside, 1, 0)

        @pl.when(inside)
        def _():
            pl.semaphore_signal(
                barrier, inc=1, device_id={"seq": me + delta}, device_id_type=MESH
            )

    mine = pl.ds(pl.multiple_of(k * half, 128), half)
    weights = [
        pltpu.make_async_copy(src, dst, w_sem.at[index])
        for index, (src, dst) in enumerate((
            (wq_hbm.at[:, mine], wq), (wk_hbm.at[:, mine], wk), (wv_hbm.at[:, mine], wv),
            (wo_hbm, wo), (wg_hbm, wg),
        ))
    ]
    for copy in weights[:3]:
        copy.start()
    for copy in small[2:]:
        copy.start()
    for copy in weights[3:]:
        copy.start()

    def place_of(section, core, part):
        if section == OWN:
            return core * rows + part * piece
        if section == LAST:
            return 6 * rows + part * piece
        return (section * 2 + part // 2) * rows + core * 2 * piece + part % 2 * piece

    def move(event, part, source, target, section, core):
        def block(where):
            low_row = place_of(where, core, part)
            return xb.at[pl.ds(pl.multiple_of(low_row, 16), piece)]

        return pltpu.make_async_remote_copy(
            src_ref=block(source),
            dst_ref=block(section),
            send_sem=send_sem.at[event, part],
            recv_sem=recv_sem.at[event, part],
            device_id={"seq": target},
            device_id_type=MESH,
        )

    sends = {
        S: (me >= 0, OWN, sibling, OWN),
        A: (me + 4 < n, OWN, me + 4, FAR),
        B: (p < 2, OWN, me + 2, NEAR),
        D: (me >= 2, NEAR, sibling, NEAR),
        E: (upper, FAR, sibling, FAR),
        F: (upper & right, FAR, me - 2, NEAR),
        H: ((k == 1) & (me >= 2) & (me + 4 < n), NEAR, me + 4, LAST),
        I: ((k == 1) & (me >= 6), LAST, sibling, LAST),
    }
    receipts = {
        S: (me >= 0, OWN),
        A: (upper, FAR),
        B: (right, NEAR),
        D: (me >= 2, NEAR),
        E: (upper, FAR),
        F: (upper & (p < 2), NEAR),
        H: ((k == 1) & (me >= 6), LAST),
        I: ((k == 0) & (me >= 6), LAST),
    }

    def start(event, part):
        condition, source, target, section = sends[event]

        @pl.when(condition)
        def _():
            move(event, part, source, target, section, k).start()

    def wait_sent(event, part):
        condition, source, target, section = sends[event]

        @pl.when(condition)
        def _():
            move(event, part, source, target, section, k).wait_send()

    def wait_here(event, part):
        condition, section = receipts[event]
        core = 1 - k if event in (S, D, E, I) else k

        @pl.when(condition)
        def _():
            move(event, part, section, sibling, section, core).wait_recv()

    starts = pltpu.make_async_remote_copy(
        src_ref=start_ref.at[k],
        dst_ref=start_ref.at[k],
        send_sem=start_sem.at[0],
        recv_sem=start_sem.at[1],
        device_id={"seq": sibling},
        device_id_type=MESH,
    )

    small[0].wait()
    gain = na_ref[...]
    for part in range(PIECES):
        frames[part].wait()
        low_row = pl.multiple_of(place_of(OWN, k, part), 16)
        xb[pl.ds(low_row, piece), :] = layer_norm(
            x_ref[part * piece:(part + 1) * piece, :].astype(F32), gain
        ).astype(BF16)
        if part == 0:
            pl.semaphore_wait(barrier, peers)
        start(A, part)
        start(B, part)
        start(S, part)
        if part == 0:
            small[1].wait()
            starts.start()

    @pl.when(me < 2)
    def _():
        xb[4 * rows:6 * rows, :] = jnp.zeros((2 * rows, width), BF16)

    @pl.when(me < 4)
    def _():
        xb[2 * rows:4 * rows, :] = jnp.zeros((2 * rows, width), BF16)

    @pl.when(me < 6)
    def _():
        xb[6 * rows:7 * rows, :] = jnp.zeros((rows, width), BF16)

    lane = lax.broadcasted_iota(jnp.int32, (rows, 128), 1).astype(F32)
    row_index = lax.broadcasted_iota(jnp.int32, (rows, 128), 0).astype(F32)
    low = lax.broadcasted_iota(jnp.int32, (rows, 128), 1) < HD
    for tile in range(rows // 128):
        seen = lane + float(tile * 128) <= row_index
        triangle[:, tile * 128:(tile + 1) * 128] = jnp.where(seen, 0.0, FLOOR_SCORE)

    def project(core):
        span_rows = pl.ds(pl.multiple_of(core * rows, 256), rows)
        normed = xb[span_rows, :]
        query = jnp.dot(normed, wq[...], preferred_element_type=F32)
        query = query.astype(BF16).astype(F32) * (HD ** -0.5)
        wide = lax.broadcasted_iota(jnp.int32, (rows, half), 1) % 128 < HD
        place = pl.multiple_of(core * 2 * rows, 256)
        q2[pl.ds(place, rows), :] = jnp.where(wide, query, 0.0).astype(BF16)
        q2[pl.ds(place + rows, rows), :] = jnp.where(wide, 0.0, query).astype(BF16)
        kb[span_rows, :] = jnp.dot(normed, wk[...], preferred_element_type=F32).astype(BF16)
        vb[span_rows, :] = jnp.dot(normed, wv[...], preferred_element_type=F32).astype(BF16)

    for copy in weights[:3]:
        copy.wait()
    project(k)

    starts.wait_recv()
    for core in range(2):
        column = jnp.broadcast_to(start_ref[core].astype(F32), (rows, rows)).T
        startb[core * rows:(core + 1) * rows, :] = (
            column[:, :128] - ((me - k) * rows).astype(F32)
        )
    startc[...] = startb[pl.ds(pl.multiple_of(k * rows, 256), rows), :] - (k * rows).astype(F32)
    for core in range(2):
        first = startb[core * rows:(core + 1) * rows, :]
        bucket = jnp.where(first < 0.0, 4.0, jnp.floor(first * (1.0 / 128.0)))
        flags = jnp.where(lane == bucket, 1.0, 0.0).astype(BF16)
        qx[core * 2 * rows:(core * 2 + 1) * rows, :] = flags
        qx[(core * 2 + 1) * rows:(core * 2 + 2) * rows, :] = flags
        kx[core * rows:(core + 1) * rows, :] = jnp.where(
            (lane == bucket) | (lane > 4.0), 0.0, FLOOR_SCORE
        ).astype(BF16)
    head = jnp.broadcast_to(startb[0:1, :], (rows, 128))

    def remote_flags(back):
        return jnp.where(
            lane < 4.0, FLOOR_SCORE,
            jnp.where((lane == 4.0) & (back < head), FLOOR_SCORE, 0.0),
        ).astype(BF16)

    for section, distance in ((FAR, 4), (NEAR, 2)):
        for part in range(2):
            back = row_index + float(part * 2 * piece - distance * rows)
            back = jnp.where(row_index >= float(2 * piece), back + float(2 * piece), back)
            place = (section * 2 + part) * rows
            kx[place:place + rows, :] = remote_flags(back)
    kx[6 * rows:7 * rows, :] = remote_flags(row_index - float(5 * rows))

    middle = startc[...] == jnp.broadcast_to(startc[128:129, :], (rows, 128))
    for tile in range(8):
        kinds[pl.ds(tile, rows, stride=8), :] = jnp.where(middle, 1.0, 0.0)

    for part in range(PIECES):
        wait_here(S, part)
    project(1 - k)

    def attend(low_query, queries, low_key, keys, opening):
        for pair in range(own_pairs):
            cols = slice(pair * 128, (pair + 1) * 128)
            held = slice(low_query, low_query + queries)
            spot = slice(low_key, low_key + keys)
            query = jnp.concatenate([q2[held, cols], qx[held, :]], axis=1)
            key = jnp.concatenate([kb[spot, cols], kx[spot, :]], axis=1)
            scores = lax.dot_general(
                query, key, (((1,), (1,)), ((), ())), preferred_element_type=F32
            )
            if opening:
                shade = triangle[...]
                if keys > rows:
                    shade = jnp.concatenate([jnp.zeros((rows, keys - rows), F32), shade], axis=1)
                scores = scores + jnp.concatenate([shade, shade], axis=0)
            top = jnp.broadcast_to(jnp.max(scores, axis=-1, keepdims=True), (queries, 128))
            if not opening:
                before = mx[pair, held]
                top = jnp.maximum(top, before)
            weights16 = jnp.exp(scores - jnp.tile(top, (1, keys // 128))).astype(BF16)
            values = jnp.concatenate([vb[spot, cols], jnp.ones((keys, 128), BF16)], axis=1)
            summed = jnp.dot(weights16, values, preferred_element_type=F32)
            if not opening:
                summed = summed + acc[pair, held] * jnp.tile(jnp.exp(before - top), (1, 2))
            acc[pair, held] = summed
            mx[pair, held] = top

    def relay_first(part):
        wait_here(A, part)
        start(F, part)
        start(E, part)
        wait_here(B, part)

        @pl.when(right)
        def _():
            move(D, part, NEAR, sibling, NEAR, k).start()
        condition, source, target, section = sends[H]

        @pl.when(right & condition)
        def _():
            move(H, part, source, target, section, k).start()

    def relay_second(part):
        wait_here(F, part)

        @pl.when(upper & (p < 2))
        def _():
            move(D, part, NEAR, sibling, NEAR, k).start()
        condition, source, target, section = sends[H]

        @pl.when(upper & (p < 2) & condition)
        def _():
            move(H, part, source, target, section, k).start()

    def relay_third(part):
        wait_here(H, part)
        start(I, part)

    def keys_of(group):
        spot = slice(group * rows, (group + 1) * rows)
        normed = xb[spot, :]
        kb[spot, :] = jnp.dot(normed, wk[...], preferred_element_type=F32).astype(BF16)
        vb[spot, :] = jnp.dot(normed, wv[...], preferred_element_type=F32).astype(BF16)

    def arrived(event, parts):
        for part in parts:
            wait_here(event, part)

    attend(0, 2 * rows, 0, rows, True)
    relay_first(0)
    attend(2 * rows, 2 * rows, 0, 2 * rows, True)
    relay_first(1)
    relay_second(0)
    arrived(E, (0, 1))
    keys_of(2)
    relay_first(2)
    relay_second(1)
    attend(0, 2 * rows, 2 * rows, rows, False)
    attend(2 * rows, 2 * rows, 2 * rows, rows, False)
    arrived(D, (0, 1))
    relay_first(3)
    relay_second(2)
    keys_of(4)
    attend(0, 2 * rows, 4 * rows, rows, False)
    attend(2 * rows, 2 * rows, 4 * rows, rows, False)
    arrived(E, (2, 3))
    relay_second(3)
    relay_third(0)
    keys_of(3)
    attend(0, 2 * rows, 3 * rows, rows, False)
    attend(2 * rows, 2 * rows, 3 * rows, rows, False)
    arrived(D, (2, 3))
    keys_of(5)
    relay_third(1)
    attend(0, 2 * rows, 5 * rows, rows, False)
    attend(2 * rows, 2 * rows, 5 * rows, rows, False)

    def heads_copy(core, pair):
        cols = pl.ds(pair * 128, 128)
        return pltpu.make_async_remote_copy(
            src_ref=heads.at[core, :, cols],
            dst_ref=heads_in.at[:, cols],
            send_sem=heads_send.at[pair],
            recv_sem=heads_recv.at[pair],
            device_id={"seq": sibling},
            device_id_type=MESH,
        )

    def close(core):
        for pair in range(own_pairs):
            cols = slice(pair * 128, (pair + 1) * 128)
            state = acc[pair, core * 2 * rows:(core + 1) * 2 * rows]
            total = jnp.where(low, state[0:rows, 0:128], state[rows:2 * rows, 0:128])
            weight_sum = jnp.where(low, state[0:rows, 128:256], state[rows:2 * rows, 128:256])
            heads[core, :, cols] = (total / weight_sum).astype(BF16)

            @pl.when(k != core)
            def _():
                heads_copy(core, pair).start()

    relay_third(2)
    close(1)
    relay_third(3)
    arrived(I, range(PIECES))
    keys_of(6)
    attend(0, 2 * rows, 6 * rows, rows, False)
    close(0)
    weights[3].wait()
    for copy in small[2:]:
        copy.wait()
    for tile in range(pairs):
        taps[pl.ds(tile, KW, stride=8), :] = wd_ref[:, tile * 128:(tile + 1) * 128]

    def output_near(index, carry):
        cols = pl.ds(pl.multiple_of(index * half, half), half)
        here = pl.ds(pl.multiple_of(k * half, half), half)
        partial[:, cols] = x_ref[:, cols].astype(F32) + jnp.dot(
            heads[k], wo[here, cols], preferred_element_type=F32
        )
        return carry

    lax.fori_loop(0, 2, output_near, 0, unroll=True)
    for pair in range(own_pairs):
        heads_copy(1 - k, pair).wait_recv()

    def output_far(index, carry):
        cols = pl.ds(pl.multiple_of(index * half, half), half)
        there = pl.ds(pl.multiple_of((1 - k) * half, half), half)
        res[:, cols] = (
            partial[:, cols]
            + jnp.dot(heads_in[...], wo[there, cols], preferred_element_type=F32)
        ).astype(BF16)
        return carry

    lax.fori_loop(0, 2, output_far, 0, unroll=True)
    xn[...] = layer_norm(res[...].astype(F32), nc_ref[...]).astype(BF16)
    weights[4].wait()

    def unit_tile(index, carry):
        cols = pl.ds(pl.multiple_of(index * 256, 256), 256)
        gate_cols = pl.ds(pl.multiple_of(width + index * 256, 256), 256)
        normed = xn[...]
        value = jnp.dot(normed, wg[:, cols], preferred_element_type=F32)
        gate = jnp.dot(normed, wg[:, gate_cols], preferred_element_type=F32)
        gated = (value * jax.nn.sigmoid(gate)).astype(BF16)
        gb[:, cols] = gated
        middle = startc[...] == jnp.broadcast_to(startc[128:129, :], (rows, 128))
        for side in range(2):
            units = gated[:, side * 128:(side + 1) * 128].astype(F32)
            place = 32 * 8 + index * 2 + side
            planes[pl.ds(place, rows, stride=8), :] = jnp.where(middle, 0.0, units)
            planes[pl.ds(span * 8 + place, rows, stride=8), :] = jnp.where(middle, units, 0.0)
        return carry

    lax.fori_loop(0, width // 256, unit_tile, 0, unroll=True)

    rim = pltpu.make_async_remote_copy(
        src_ref=gb.at[pl.ds(rows - 32, 32)],
        dst_ref=halo,
        send_sem=halo_sem.at[0],
        recv_sem=halo_sem.at[1],
        device_id={"seq": me + 1},
        device_id_type=MESH,
    )

    @pl.when(me + 1 < n)
    def _():
        rim.start()

    block = 16

    def conv_block(index, carry):
        base = index * block

        def row(ref, place):
            return ref[pl.ds(pl.multiple_of(place * 8, 8), 8), :]

        inside = [row(kinds, base + r) > 0.5 for r in range(block)]
        total = [None] * block
        for j in range(KW - 1):
            place = base + 2 + j
            entry = jnp.where(inside[0], row(planes, span + place), row(planes, place))
            for r in range(min(j + 1, block)):
                term = entry * tap_rows[j - r]
                total[r] = term if total[r] is None else total[r] + term
        for r in range(1, block):
            total[r] = jnp.where(inside[r] == inside[0], total[r], 0.0)
        for j in range(block):
            place = base + 32 + j
            other, middle = row(planes, place), row(planes, span + place)
            for r in range(j, block):
                entry = jnp.where(inside[r], middle, other)
                total[r] = total[r] + entry * tap_rows[KW - 1 - r + j]
        for r in range(block):
            depth[pl.ds(pl.multiple_of((base + r) * 8, 8), 8), :] = total[r]
        return carry

    tap_rows = [taps[tap * 8:(tap + 1) * 8, :] for tap in range(KW)]
    lax.fori_loop(2, rows // block, conv_block, 0)

    def finish(low_row, count):
        columns = [
            depth[pl.ds(low_row * 8 + tile, count, stride=8), :] for tile in range(pairs)
        ]
        normed_depth = layer_norm(jnp.concatenate(columns, axis=1), nd_ref[...])
        out_ref[low_row:low_row + count, :] = (
            res[low_row:low_row + count, :].astype(F32)
            + normed_depth * jax.nn.sigmoid(normed_depth)
        ).astype(BF16)

    finish(32, rows - 32)

    @pl.when(me == 0)
    def _():
        halo[...] = jnp.zeros_like(halo)

    @pl.when(me > 0)
    def _():
        rim.wait_recv()

    back = lax.broadcasted_iota(jnp.int32, (32, 128), 0).astype(F32) - 32.0
    middle = back >= jnp.broadcast_to(startc[128:129, :], (32, 128))
    for tile in range(pairs):
        units = halo[:, tile * 128:(tile + 1) * 128].astype(F32)
        planes[pl.ds(tile, 32, stride=8), :] = jnp.where(middle, 0.0, units)
        planes[pl.ds(span * 8 + tile, 32, stride=8), :] = jnp.where(middle, units, 0.0)
    lax.fori_loop(0, 2, conv_block, 0)
    finish(0, 32)

    for event in range(8):
        for part in range(PIECES):
            wait_sent(event, part)
    starts.wait_send()
    for pair in range(own_pairs):
        heads_copy(1 - k, pair).wait_send()

    @pl.when(me + 1 < n)
    def _():
        rim.wait_send()


def body(
    frames_in, rec_start, norm_attn, w_query, w_key, w_value, w_out, norm_conv, w_glu, w_depth,
    norm_depth,
):
    rows, width = frames_in.shape
    half = width // 2
    own_pairs = half // 128
    hbm = pl.BlockSpec(memory_space=pl.ANY)
    tall = pltpu.VMEM((width, half), BF16)
    return pl.pallas_call(
        kernel,
        out_shape=pltpu.VMEM((rows, width), BF16),
        in_specs=[hbm] * 11,
        out_specs=pl.BlockSpec(memory_space=pltpu.VMEM),
        scratch_shapes=[
            pltpu.VMEM((7 * rows, width), BF16),
            pltpu.VMEM((4 * rows, 128), BF16),
            pltpu.VMEM((7 * rows, 128), BF16),
            tall, tall, tall,
            pltpu.VMEM((width, width), BF16),
            pltpu.VMEM((width, 2 * width), BF16),
            pltpu.VMEM((rows, width), BF16),
            pltpu.VMEM((4 * rows, half), BF16),
            pltpu.VMEM((7 * rows, half), BF16),
            pltpu.VMEM((7 * rows, half), BF16),
            pltpu.VMEM((rows, rows), F32),
            pltpu.VMEM((2 * rows, 128), F32),
            pltpu.VMEM((rows, 128), F32),
            pltpu.VMEM((own_pairs, 4 * rows, 128), F32),
            pltpu.VMEM((own_pairs, 4 * rows, 256), F32),
            pltpu.VMEM((2, rows, half), BF16),
            pltpu.VMEM((rows, half), BF16),
            pltpu.VMEM((rows, width), F32),
            pltpu.VMEM((rows, width), BF16),
            pltpu.VMEM((rows, width), BF16),
            pltpu.VMEM((32, width), BF16),
            pltpu.VMEM((2 * (rows + 32) * 8, 128), F32),
            pltpu.VMEM((rows * 8, 128), F32),
            pltpu.VMEM((KW * 8, 128), F32),
            pltpu.VMEM((rows, width), BF16),
            pltpu.VMEM((2, 1, rows), jnp.int32),
            pltpu.VMEM((1, width), F32),
            pltpu.VMEM((1, width), F32),
            pltpu.VMEM((1, width), F32),
            pltpu.VMEM((KW, width), F32),
            pltpu.VMEM((rows * 8, 128), F32),
            pltpu.SemaphoreType.DMA((5,)),
            pltpu.SemaphoreType.DMA((PIECES + 5,)),
            pltpu.SemaphoreType.DMA((8, PIECES)),
            pltpu.SemaphoreType.DMA((8, PIECES)),
            pltpu.SemaphoreType.DMA((2,)),
            pltpu.SemaphoreType.DMA((2,)),
            pltpu.SemaphoreType.DMA((own_pairs,)),
            pltpu.SemaphoreType.DMA((own_pairs,)),
        ],
        compiler_params=pltpu.CompilerParams(
            collective_id=0, has_side_effects=True, vmem_limit_bytes=60 * 1024 * 1024
        ),
    )(
        frames_in, rec_start.reshape(1, rows), norm_attn.reshape(1, width),
        norm_conv.reshape(1, width), norm_depth.reshape(1, width), w_depth,
        w_query, w_key, w_value, w_out, w_glu,
    )


def solution(mesh):
    return jax.shard_map(
        body,
        mesh=mesh,
        in_specs=(P(("groups", "seq"), None), P(("groups", "seq"))) + (P(),) * 9,
        out_specs=P(("groups", "seq"), None),
        check_vma=False,
    )
```
